32 devices in a mesh: grp: 2 (over x), tm: 16 (over z, y, core).
Axes of the slice: x: 2, y: 2, z: 4, core: 2. Of those that a mesh axis runs over, the one named last changes fastest.
Arguments:
- waveform: float32 [262144], P(('grp', 'tm')), parts along dimension 0, may hold values from -8 to 8
- enc_weight: float32 [16, 256], replicated, may hold values from -1.5 to 1.5
- intra_qkv: bfloat16 [256, 768], replicated, may hold values from -3 to 3
- intra_out: bfloat16 [256, 256], replicated, may hold values from -0.375 to 0.375
- intra_up: bfloat16 [256, 1024], replicated, may hold values from -0.375 to 0.375
- intra_down: bfloat16 [1024, 256], replicated, may hold values from -0.1875 to 0.1875
- inter_qkv: bfloat16 [256, 768], replicated, may hold values from -3 to 3
- inter_out: bfloat16 [256, 256], replicated, may hold values from -0.375 to 0.375
- inter_up: bfloat16 [256, 1024], replicated, may hold values from -0.375 to 0.375
- inter_down: bfloat16 [1024, 256], replicated, may hold values from -0.1875 to 0.1875
- mask_weight: bfloat16 [256, 512], replicated, may hold values from -0.375 to 0.375
Outputs:
- separated: bfloat16 [2, 32768, 256], P(None, ('grp', 'tm')), parts along dimension 1
The draws below stay inside these ranges and needn't reach their ends.
There are 2 independent parts, one for each index of `grp`. The reference program is written for one: setup_inputs(seed, part) draws one part's arguments, and reference() takes and returns one part's arrays. A program takes and returns all parts, laid end to end along the dimension named above; an argument that names none is the same for every part. Nothing has to cross between parts.
All inputs are finite; a program needn't handle non-finite values.
Results may differ from the reference program's by a relative error of at most 0.011.
Values may be sent and summed in bfloat16 or wider, within the bound.
No kernel may reach another device: no remote copies, remote signals or barrier semaphores. Data moves between devices by JAX's collectives and lax.ppermute only.
A program may use at most 192 MiB of HBM per device.

```python
import math
import jax
import jax.numpy as jnp
from jax import lax

D = 256
HEADS = 8
HEAD = 32
FFN = 1024
TAPS = 16
HOP = 8
HALF = 128
FRAMES = 16384
SAMPLES = 131072
SEGMENTS = 128


def draw_waveform(key, part):
    key_noise, key_level = jax.random.split(key)
    levels = jnp.exp(jax.random.uniform(key_level, (SAMPLES // 256,), jnp.float32, -1.5, 1.5))
    noise = jax.random.normal(key_noise, (SAMPLES // 256, 256), jnp.float32)
    return jnp.clip(noise * levels[:, None], -8.0, 8.0).reshape(SAMPLES)


def draw_projection(key, model_width):
    key_main = jax.random.fold_in(key, 0)
    noise = jax.random.normal(key_main, (model_width, 3 * model_width), jnp.float32) / math.sqrt(model_width)
    result = noise
    return jnp.clip(result, -3.0, 3.0)


def draw_intra_qkv(key, part):
    return draw_projection(jax.random.fold_in(key, 11), D).astype(jnp.bfloat16)


def draw_inter_qkv(key, part):
    return draw_projection(jax.random.fold_in(key, 23), D).astype(jnp.bfloat16)


def bell_draw(rng, dims, width, limit, held_as=jnp.bfloat16):
    return jnp.clip(width * jax.random.normal(rng, dims, jnp.float32), -limit, limit).astype(held_as)


def setup_inputs(seed: int = 0, part: int = 0) -> dict:
    keys = jax.random.split(jax.random.key(seed), 12)
    own_keys = jax.random.split(jax.random.fold_in(keys[11], part), 12)
    waveform = draw_waveform(jax.random.fold_in(jax.random.fold_in(keys[11], part), 71), part)
    enc_weight = bell_draw(keys[1], (TAPS, D), TAPS ** -0.5, 1.5, jnp.float32)
    intra_qkv = draw_intra_qkv(jax.random.fold_in(keys[11], 71), part)
    intra_out = bell_draw(keys[3], (D, D), D ** -0.5, 0.375)
    intra_up = bell_draw(keys[4], (D, FFN), D ** -0.5, 0.375)
    intra_down = bell_draw(keys[5], (FFN, D), FFN ** -0.5, 0.1875)
    inter_qkv = draw_inter_qkv(jax.random.fold_in(keys[11], 71), part)
    inter_out = bell_draw(keys[7], (D, D), D ** -0.5, 0.375)
    inter_up = bell_draw(keys[8], (D, FFN), D ** -0.5, 0.375)
    inter_down = bell_draw(keys[9], (FFN, D), FFN ** -0.5, 0.1875)
    mask_weight = bell_draw(keys[10], (D, 2 * D), D ** -0.5, 0.375)
    return {"waveform": waveform, "enc_weight": enc_weight, "intra_qkv": intra_qkv, "intra_out": intra_out, "intra_up": intra_up, "intra_down": intra_down, "inter_qkv": inter_qkv, "inter_out": inter_out, "inter_up": inter_up, "inter_down": inter_down, "mask_weight": mask_weight}


def rounded(values):
    return lax.optimization_barrier(values.astype(jnp.bfloat16))

def layer_norm(values):
    values = values.astype(jnp.float32)
    centred = values - lax.optimization_barrier(jnp.mean(values, axis=-1, keepdims=True))
    spread = lax.optimization_barrier(jnp.mean(centred * centred, axis=-1, keepdims=True))
    return centred * lax.rsqrt(spread + 1e-05)

def project(values, weight):
    flattened = values.reshape(-1, values.shape[-1])
    result = jnp.dot(flattened, weight, preferred_element_type=jnp.float32)
    return result.reshape(values.shape[:-1] + (weight.shape[1],))

def attend(queries, key_rows, value_rows, seq_first):
    full_shape = queries.shape
    split_shape = full_shape[:-1] + (HEADS, HEAD)
    query_heads = queries.reshape(split_shape).astype(jnp.float32)
    key_heads = key_rows.reshape(split_shape).astype(jnp.float32)
    value_heads = value_rows.reshape(split_shape).astype(jnp.float32)
    if seq_first:
        score_form = 'lbhe,kbhe->bhlk'
        weigh_form = 'bhlk,kbhe->lbhe'
    else:
        score_form = 'blhe,bkhe->bhlk'
        weigh_form = 'bhlk,bkhe->blhe'
    scores = jnp.einsum(score_form, query_heads, key_heads) * HEAD ** (-0.5)
    probs = jax.nn.softmax(scores, axis=-1).astype(jnp.bfloat16)
    mixture = jnp.einsum(weigh_form, probs.astype(jnp.float32), value_heads)
    return mixture.astype(jnp.bfloat16).reshape(full_shape)

def transformer_layer(tokens, weights, seq_first):
    qkv_weight, out_weight, up_weight, down_weight = weights
    model_width = tokens.shape[-1]
    normed = layer_norm(tokens).astype(jnp.bfloat16)
    triple = project(normed, qkv_weight).astype(jnp.bfloat16)
    attended = attend(triple[..., :model_width], triple[..., model_width:2 * model_width], triple[..., 2 * model_width:], seq_first)
    after_attention = rounded(tokens.astype(jnp.float32) + project(attended, out_weight))
    normed_again = layer_norm(after_attention).astype(jnp.bfloat16)
    hidden = jax.nn.relu(project(normed_again, up_weight)).astype(jnp.bfloat16)
    return (after_attention.astype(jnp.float32) + project(hidden, down_weight)).astype(jnp.bfloat16)

def reference(waveform, enc_weight, intra_qkv, intra_out, intra_up, intra_down, inter_qkv, inter_out, inter_up, inter_down, mask_weight):
    blocks = waveform.reshape(FRAMES, HOP)
    following = jnp.concatenate([blocks[1:], jnp.zeros((1, HOP), blocks.dtype)], axis=0)
    framed = jnp.concatenate([blocks, following], axis=1)
    encoded = rounded(jax.nn.relu(jnp.dot(framed, enc_weight, precision=lax.Precision.HIGHEST, preferred_element_type=jnp.float32)))
    padded = jnp.concatenate([encoded, jnp.zeros((HALF, D), jnp.bfloat16)], axis=0)
    padded = padded.reshape(SEGMENTS + 1, HALF, D)
    segmented = jnp.concatenate([padded[:-1], padded[1:]], axis=1)
    intra_weights = (intra_qkv, intra_out, intra_up, intra_down)
    inter_weights = (inter_qkv, inter_out, inter_up, inter_down)

    def within_one(segment_rows):
        return transformer_layer(segment_rows[None], intra_weights, False)[0]
    within = lax.map(within_one, segmented)
    by_position = jnp.swapaxes(within, 0, 1)

    def across_one(position_rows):
        return transformer_layer(position_rows[:, None, :], inter_weights, True)[:, 0, :]
    across = lax.map(across_one, by_position)
    halves = jnp.swapaxes(across, 0, 1).reshape(SEGMENTS, 2, HALF, D)
    lagged = jnp.concatenate([jnp.zeros((1, HALF, D), jnp.bfloat16), halves[:-1, 1]], axis=0)
    combined = rounded(halves[:, 0].astype(jnp.float32) + lagged.astype(jnp.float32)).reshape(FRAMES, D)
    activated = combined.astype(jnp.float32)
    activated = jnp.where(activated > 0, activated, 0.25 * activated).astype(jnp.bfloat16)
    mask_values = jax.nn.relu(jnp.dot(activated, mask_weight, preferred_element_type=jnp.float32))
    mask_values = mask_values.reshape(FRAMES, 2, D)
    separated = (mask_values * encoded.astype(jnp.float32)[:, None, :]).astype(jnp.bfloat16)
    return jnp.transpose(separated, (1, 0, 2))
```

```python
import math

import jax
import jax.numpy as jnp
from jax import lax
from jax.experimental import pallas as pl
from jax.experimental.pallas import tpu as pltpu
from jax.sharding import PartitionSpec as P

HEADS = 8
HEAD = 32
HOP = 8
HALF = 128


def shifted(value, axis, steps):
    count = lax.axis_size(axis)
    leading, last = (max(0, -steps), min(count, count - steps))
    return lax.ppermute(value, axis, [(source, source + steps) for source in range(leading, last)])


def rounded(values):
    return lax.optimization_barrier(values.astype(jnp.bfloat16))


def layer_norm(values):
    values = values.astype(jnp.float32)
    centred = values - jnp.mean(values, axis=-1, keepdims=True)
    spread = jnp.mean(centred * centred, axis=-1, keepdims=True)
    return centred * lax.rsqrt(spread + 1e-05)


def project(values, weight):
    flattened = values.reshape(-1, values.shape[-1])
    result = jnp.dot(flattened, weight, preferred_element_type=jnp.float32)
    return result.reshape(values.shape[:-1] + (weight.shape[1],))


def attend(queries, key_rows, value_rows, seq_first):
    full_shape = queries.shape
    split_shape = full_shape[:-1] + (HEADS, HEAD)
    query_heads = queries.reshape(split_shape)
    key_heads = key_rows.reshape(split_shape)
    value_heads = value_rows.reshape(split_shape)
    if seq_first:
        score_form = "lbhe,kbhe->bhlk"
        weigh_form = "bhlk,kbhe->lbhe"
    else:
        score_form = "blhe,bkhe->bhlk"
        weigh_form = "bhlk,bkhe->blhe"
    scores = jnp.einsum(
        score_form, query_heads, key_heads, preferred_element_type=jnp.float32
    ) * HEAD ** (-0.5)
    probs = jax.nn.softmax(scores, axis=-1).astype(jnp.bfloat16)
    mixture = jnp.einsum(weigh_form, probs, value_heads, preferred_element_type=jnp.float32)
    return mixture.astype(jnp.bfloat16).reshape(full_shape)


def transformer_layer(tokens, weights, seq_first):
    qkv_weight, out_weight, up_weight, down_weight = weights
    model_width = tokens.shape[-1]
    normed = layer_norm(tokens).astype(jnp.bfloat16)
    triple = project(normed, qkv_weight).astype(jnp.bfloat16)
    attended = attend(
        triple[..., :model_width],
        triple[..., model_width : 2 * model_width],
        triple[..., 2 * model_width :],
        seq_first,
    )
    after_attention = rounded(tokens.astype(jnp.float32) + project(attended, out_weight))
    normed_again = layer_norm(after_attention).astype(jnp.bfloat16)
    hidden = jax.nn.relu(project(normed_again, up_weight)).astype(jnp.bfloat16)
    return (after_attention.astype(jnp.float32) + project(hidden, down_weight)).astype(jnp.bfloat16)


def encode(framed, enc_weight):
    return rounded(
        jax.nn.relu(
            jnp.dot(
                framed,
                enc_weight,
                precision=lax.Precision.HIGHEST,
                preferred_element_type=jnp.float32,
            )
        )
    )


def local(
    waveform,
    enc_weight,
    intra_qkv,
    intra_out,
    intra_up,
    intra_down,
    inter_qkv,
    inter_out,
    inter_up,
    inter_down,
    mask_weight,
):
    model_width = enc_weight.shape[1]
    frames_here = waveform.shape[0] // HOP
    blocks = waveform.reshape(frames_here, HOP)
    first_block = shifted(blocks[:1], "tm", -1)
    following = jnp.concatenate([blocks[1:], first_block], axis=0)
    framed = jnp.concatenate([blocks, following], axis=1)
    encoded = encode(framed, enc_weight)
    frame_edge = shifted(encoded[:HALF], "tm", -1)
    padded = jnp.concatenate([encoded, frame_edge], axis=0)
    segment_total = frames_here // HALF
    stacked = padded.reshape(segment_total + 1, HALF, model_width)
    segmented = jnp.concatenate([stacked[:-1], stacked[1:]], axis=1)
    intra_weights = (intra_qkv, intra_out, intra_up, intra_down)
    inter_weights = (inter_qkv, inter_out, inter_up, inter_down)
    within = transformer_layer(segmented, intra_weights, False)
    within = within.reshape(segment_total, 2, HALF, model_width)
    pieces = lax.all_to_all(within, "tm", split_axis=2, concat_axis=0, tiled=True)
    row_total, item_count, spot_count, feature_count = pieces.shape
    flattened = pieces.reshape(row_total, item_count * spot_count, feature_count)
    result = transformer_layer(flattened, inter_weights, True)
    across = result.reshape(row_total, item_count, spot_count, feature_count)
    returned = lax.all_to_all(across, "tm", split_axis=0, concat_axis=2, tiled=True)
    tail_half = shifted(returned[-1:, 1], "tm", 1)
    lagged = jnp.concatenate([tail_half, returned[:-1, 1]], axis=0)
    combined = rounded(returned[:, 0].astype(jnp.float32) + lagged.astype(jnp.float32))
    combined = combined.reshape(frames_here, model_width)
    activated = combined.astype(jnp.float32)
    activated = jnp.where(activated > 0, activated, 0.25 * activated).astype(jnp.bfloat16)
    mask_values = jax.nn.relu(jnp.dot(activated, mask_weight, preferred_element_type=jnp.float32))
    mask_values = mask_values.reshape(frames_here, 2, model_width)
    separated = (mask_values * encoded.astype(jnp.float32)[:, None, :]).astype(jnp.bfloat16)
    return jnp.transpose(separated, (1, 0, 2))


LANES = 128
WITHIN_BATCH = 4
SCORE_SCALE = math.log2(math.e) * HEAD ** (-0.5)


def normalise(values):
    mean = jnp.sum(values, axis=-1, keepdims=True) * (1.0 / values.shape[-1])
    centred = values - mean
    spread = jnp.sum(centred * centred, axis=-1, keepdims=True) * (1.0 / values.shape[-1])
    return centred * lax.rsqrt(spread + 1e-05)


def round_trip(values):
    return values.astype(jnp.bfloat16).astype(jnp.float32)


def matmul(left, right):
    return jnp.dot(left, right, preferred_element_type=jnp.float32)


def put(ref, rows, value, *lead):
    for block in range(value.shape[1] // LANES):
        ref[(*lead, block, rows, slice(None))] = value[:, block * LANES : (block + 1) * LANES]


def get(ref, rows):
    return jnp.concatenate([ref[block, rows, :] for block in range(ref.shape[0])], axis=1)


def attend_rows(batch):
    group = LANES // HEAD
    work = []
    for queries, keys, values in batch:
        lane_head = lax.broadcasted_iota(jnp.int32, (queries.shape[0], LANES), 1) // HEAD
        for half in range(queries.shape[1] // LANES):
            columns = slice(half * LANES, (half + 1) * LANES)
            part = queries[:, columns]
            spread = [jnp.where(lane_head == head, part, 0.0) for head in range(group)]
            spread = jnp.concatenate(spread, axis=0).astype(jnp.bfloat16)
            work.append((matmul(spread, keys[columns, :]), values[:, columns]))
    shares = []
    for scores, part in work:
        peak = jnp.max(scores, axis=-1, keepdims=True)
        weights = jnp.exp2((scores - peak) * SCORE_SCALE)
        total = jnp.sum(weights, axis=-1, keepdims=True)
        shares.append((weights.astype(jnp.bfloat16), total, part))
    mixed = [matmul(weights, part) * (1.0 / total) for weights, total, part in shares]
    results = []
    for queries, _, _ in batch:
        rows = queries.shape[0]
        lane_head = lax.broadcasted_iota(jnp.int32, (rows, LANES), 1) // HEAD
        halves = []
        for half in range(queries.shape[1] // LANES):
            block = mixed.pop(0)
            result = block[:rows]
            for head in range(1, group):
                result = jnp.where(lane_head == head, block[head * rows : (head + 1) * rows], result)
            halves.append(result)
        results.append(jnp.concatenate(halves, axis=1))
    return results


def finish_rows(tokens, attended, out_weight, up_weight, down_weight):
    after = round_trip(tokens + matmul(attended, out_weight))
    normed = normalise(after).astype(jnp.bfloat16)
    hidden = jnp.maximum(matmul(normed, up_weight), 0.0).astype(jnp.bfloat16)
    return round_trip(after + matmul(hidden, down_weight))


def core_kernel(
    place_ref,
    wave_ref,
    enc_ref,
    intra_qkv,
    intra_out,
    intra_up,
    intra_down,
    inter_qkv,
    inter_out,
    inter_up,
    inter_down,
    act_ref,
    own_ref,
    band32,
    band,
    batch,
    normed,
    keys,
    values,
    query_x,
    queries,
    tokens,
    attended,
    middle,
    inter_q,
    inter_k,
    inter_v,
    turned_out,
    lag,
):
    width = enc_ref.shape[1]
    place = place_ref[0]
    rows_total = wave_ref.shape[0] - 16
    segments = rows_total // 8
    reach = HALF // 2 + HOP
    spill = LANES - reach

    band32[...] = jnp.zeros_like(band32)
    filters = enc_ref[...]
    high = round_trip(filters)
    low = round_trip(filters - high)
    for step in range(8):
        columns = slice(step * width, (step + 1) * width)
        for piece in range(2):
            sample = 8 * step + 8 * piece
            rows = slice(8 * piece, 8 * piece + 8)
            band32[sample : sample + 8, columns] = high[rows]
            band32[LANES + sample : LANES + sample + 8, columns] = high[rows]
            where = LANES + reach + sample if sample < spill else reach + sample - spill
            band32[where : where + 8, columns] = low[rows]
    band[...] = band32[...].astype(jnp.bfloat16)

    per_chunk = 64
    lane = lax.broadcasted_iota(jnp.int32, (per_chunk, LANES), 1)

    def encode_chunk(chunk, carry):
        start = pl.multiple_of(chunk * per_chunk, per_chunk)
        here = wave_ref[pl.ds(start, per_chunk), :]
        after = wave_ref[pl.ds(start + 1, per_chunk), :]
        turned = jnp.where(lane < 64, pltpu.roll(here, 64, 1), pltpu.roll(after, 64, 1))
        stacked = []
        for samples in (here, turned):
            coarse = round_trip(samples)
            fine = samples - coarse
            first = jnp.where(lane < reach, coarse, pltpu.roll(coarse, reach - spill, 1))
            second = jnp.where(lane < reach, fine, pltpu.roll(coarse, reach, 1))
            stacked.append(jnp.concatenate([first, second], axis=1))
        framed = jnp.concatenate(stacked, axis=0).astype(jnp.bfloat16)
        for step in range(8):
            columns = slice(step * width, (step + 1) * width)
            coded = round_trip(jnp.maximum(matmul(framed, band[:, columns]), 0.0))
            ready = normalise(coded)
            for half in range(2):
                rows = slice(half * per_chunk, (half + 1) * per_chunk)
                batch[8 * half + step] = coded[rows]
                normed[:, 8 * half + step] = ready[rows].reshape(8, 8, width)
        query_x[pl.ds(start, per_chunk), :] = batch[place]

        @pl.when(chunk == place)
        def _():
            own_ref[...] = batch[...].astype(jnp.bfloat16)

        both = normed[...].reshape(8 * HALF, width).astype(jnp.bfloat16)
        target = pl.ds(pl.multiple_of(chunk * 8 * HALF, 8 * HALF), 8 * HALF)
        keys[:, target] = matmul(both, intra_qkv[:, width : 2 * width]).astype(jnp.bfloat16).T
        values[target, :] = matmul(both, intra_qkv[:, 2 * width :]).astype(jnp.bfloat16)
        return carry

    lax.fori_loop(0, segments // 8, encode_chunk, 0)
    keys[:, segments * HALF :] = jnp.zeros((width, HALF), jnp.bfloat16)
    values[segments * HALF :, :] = jnp.zeros((HALF, width), jnp.bfloat16)
    query_x[rows_total : rows_total + 8, :] = jnp.zeros((8, width), jnp.float32)
    queries[rows_total : rows_total + 8, :] = jnp.zeros((8, width), jnp.float32)

    def query_chunk(chunk, carry):
        rows = pl.ds(pl.multiple_of(chunk * 256, 256), 256)
        ready = normalise(query_x[rows, :]).astype(jnp.bfloat16)
        queries[rows, :] = round_trip(matmul(ready, intra_qkv[:, :width]))
        return carry

    lax.fori_loop(0, rows_total // 256, query_chunk, 0)

    def within_chunk(chunk, carry):
        batch, targets = [], []
        for inner in range(WITHIN_BATCH):
            segment = chunk * WITHIN_BATCH + inner
            rows = pl.ds(pl.multiple_of(segment * 8, 8), 16)
            span = pl.ds(pl.multiple_of(segment * HALF, HALF), 2 * HALF)
            target = pl.ds(pl.multiple_of(segment * 16, 16), 16)
            tokens[target, :] = query_x[rows, :]
            batch.append((queries[rows, :], keys.at[:, span], values.at[span, :]))
            targets.append(target)
        for target, result in zip(targets, attend_rows(batch)):
            attended[target, :] = result.astype(jnp.bfloat16)
        return carry

    lax.fori_loop(0, segments // WITHIN_BATCH, within_chunk, 0)

    positions = 16
    row_count = positions * segments

    def within_finish(chunk, carry):
        rows = pl.ds(pl.multiple_of(chunk * 256, 256), 256)
        put(middle, rows, finish_rows(tokens[rows, :], attended[rows, :], intra_out[...], intra_up[...], intra_down[...]))
        return carry

    lax.fori_loop(0, row_count // 256, within_finish, 0)

    def turn(chunk, carry):
        for inner in range(2):
            spot = chunk * 2 + inner
            rows = pl.ds(pl.multiple_of(spot * segments, segments), segments)
            picked = get(middle, pl.ds(spot, segments, stride=positions))
            tokens[rows, :] = picked
            triple = matmul(normalise(picked).astype(jnp.bfloat16), inter_qkv[...])
            inter_q[rows, :] = round_trip(triple[:, :width])
            inter_k[:, rows] = triple[:, width : 2 * width].astype(jnp.bfloat16).T
            inter_v[rows, :] = triple[:, 2 * width :].astype(jnp.bfloat16)
        return carry

    lax.fori_loop(0, positions // 2, turn, 0)

    def across_chunk(spot, carry):
        rows = pl.ds(pl.multiple_of(spot * segments, segments), segments)
        (result,) = attend_rows([(inter_q[rows, :], inter_k.at[:, rows], inter_v.at[rows, :])])
        attended[rows, :] = result.astype(jnp.bfloat16)
        return carry

    lax.fori_loop(0, positions, across_chunk, 0)

    def across_finish(chunk, carry):
        rows = pl.ds(pl.multiple_of(chunk * 256, 256), 256)
        put(middle, rows, finish_rows(tokens[rows, :], attended[rows, :], inter_out[...], inter_up[...], inter_down[...]))
        return carry

    lax.fori_loop(0, row_count // 256, across_finish, 0)

    lag[0:8, :] = jnp.zeros((8, width), jnp.float32)
    for spot in range(positions // 2):
        lag[8 : 8 + segments, :] = get(middle, pl.ds((spot + positions // 2) * segments, segments))
        combined = round_trip(get(middle, pl.ds(spot * segments, segments)) + lag[7 : 7 + segments, :])
        active = jnp.where(combined > 0, combined, 0.25 * combined)
        put(turned_out, pl.ds(spot, segments, stride=positions // 2), active)
    act_ref[...] = get(turned_out, slice(None)).astype(jnp.bfloat16)


def mask_kernel(act_ref, own_ref, weight_ref, out_ref, stage):
    width = own_ref.shape[-1]
    steps = own_ref.shape[0]
    rows = own_ref.shape[1]
    for step in range(steps):
        scale = own_ref[step].astype(jnp.float32)
        for speaker in range(2):
            columns = slice(speaker * width, (speaker + 1) * width)
            mask = jnp.maximum(matmul(act_ref[step], weight_ref[:, columns]), 0.0)
            put(stage, pl.ds(step, rows, stride=steps), mask * scale, speaker)
    for speaker in range(2):
        out_ref[speaker] = get(stage.at[speaker], slice(None)).astype(jnp.bfloat16)


def core_call(place, wave, enc_weight, *rest):
    *weights, own_rows = rest
    width = enc_weight.shape[1]
    rows_total = wave.shape[0] - 16
    segments = rows_total // 8
    row_count = 16 * segments
    vmem = pl.BlockSpec(memory_space=pltpu.VMEM)
    return pl.pallas_call(
        core_kernel,
        out_shape=(
            jax.ShapeDtypeStruct((rows_total, width), jnp.bfloat16),
            jax.ShapeDtypeStruct((16, own_rows, width), jnp.bfloat16),
        ),
        in_specs=[pl.BlockSpec(memory_space=pltpu.SMEM)] + [vmem] * 10,
        out_specs=(vmem, vmem),
        scratch_shapes=[
            pltpu.VMEM((2 * LANES, 8 * width), jnp.float32),
            pltpu.VMEM((2 * LANES, 8 * width), jnp.bfloat16),
            pltpu.VMEM((16, own_rows, width), jnp.float32),
            pltpu.VMEM((8, 16, 8, width), jnp.float32),
            pltpu.VMEM((width, (segments + 1) * HALF), jnp.bfloat16),
            pltpu.VMEM(((segments + 1) * HALF, width), jnp.bfloat16),
            pltpu.VMEM((rows_total + 8, width), jnp.float32),
            pltpu.VMEM((rows_total + 8, width), jnp.float32),
            pltpu.VMEM((row_count, width), jnp.float32),
            pltpu.VMEM((row_count, width), jnp.bfloat16),
            pltpu.VMEM((width // LANES, row_count, LANES), jnp.float32),
            pltpu.VMEM((row_count, width), jnp.float32),
            pltpu.VMEM((width, row_count), jnp.bfloat16),
            pltpu.VMEM((row_count, width), jnp.bfloat16),
            pltpu.VMEM((width // LANES, rows_total, LANES), jnp.float32),
            pltpu.VMEM((segments + 8, width), jnp.float32),
        ],
        compiler_params=pltpu.CompilerParams(vmem_limit_bytes=60 * 1024 * 1024),
        name="core",
    )(place, wave, enc_weight, *weights)


def gather_doubling(value, axis):
    count = lax.axis_size(axis)
    index = lax.axis_index(axis)
    held = value[None]
    bit = count // 2
    while bit:
        other = lax.ppermute(held, axis, [(source, source ^ bit) for source in range(count)])
        upper = (index // bit) % 2
        first = jnp.where(upper == 0, held, other)
        second = jnp.where(upper == 0, other, held)
        held = jnp.stack([first, second], axis=1).reshape((-1,) + value.shape)
        bit //= 2
    return held.reshape((-1,) + value.shape[1:])


def local_gathered(
    waveform,
    enc_weight,
    intra_qkv,
    intra_out,
    intra_up,
    intra_down,
    inter_qkv,
    inter_out,
    inter_up,
    inter_down,
    mask_weight,
):
    width = enc_weight.shape[1]
    count = lax.axis_size("tm")
    samples = waveform.reshape(-1, LANES)
    gathered = gather_doubling(samples, "tm")
    wave = jnp.concatenate([gathered, jnp.zeros((16, LANES), jnp.float32)], axis=0)
    own_rows = samples.shape[0]
    place = lax.axis_index("tm").reshape(1)
    weights = (intra_qkv, intra_out, intra_up, intra_down, inter_qkv, inter_out, inter_up, inter_down)
    act, own = core_call(place, wave, enc_weight, *weights, own_rows)
    pieces = act.reshape(count, own_rows, width)
    vmem = pl.BlockSpec(memory_space=pltpu.VMEM)
    received = lax.all_to_all(pieces, "tm", split_axis=0, concat_axis=0, tiled=True)
    return pl.pallas_call(
        mask_kernel,
        out_shape=jax.ShapeDtypeStruct((2, 16 * own_rows, width), jnp.bfloat16),
        in_specs=[vmem] * 3,
        out_specs=vmem,
        scratch_shapes=[pltpu.VMEM((2, width // LANES, 16 * own_rows, LANES), jnp.float32)],
        compiler_params=pltpu.CompilerParams(vmem_limit_bytes=32 * 1024 * 1024),
        name="mask",
    )(received, own, mask_weight)


def solution(mesh):
    body = local_gathered if mesh.shape["tm"] == 16 else local
    return jax.shard_map(
        body,
        mesh=mesh,
        in_specs=(P(("grp", "tm")), P(), P(), P(), P(), P(), P(), P(), P(), P(), P()),
        out_specs=P(None, ("grp", "tm"), None),
        check_vma=False,
    )
```

```python
import math

import jax
import jax.numpy as jnp
from jax import lax
from jax.experimental import pallas as pl
from jax.experimental.pallas import tpu as pltpu
from jax.sharding import PartitionSpec as P

HEADS = 8
HEAD = 32
HOP = 8
HALF = 128


def shifted(value, axis, steps):
    count = lax.axis_size(axis)
    leading, last = (max(0, -steps), min(count, count - steps))
    return lax.ppermute(value, axis, [(source, source + steps) for source in range(leading, last)])


def rounded(values):
    return lax.optimization_barrier(values.astype(jnp.bfloat16))


def layer_norm(values):
    values = values.astype(jnp.float32)
    centred = values - jnp.mean(values, axis=-1, keepdims=True)
    spread = jnp.mean(centred * centred, axis=-1, keepdims=True)
    return centred * lax.rsqrt(spread + 1e-05)


def project(values, weight):
    flattened = values.reshape(-1, values.shape[-1])
    result = jnp.dot(flattened, weight, preferred_element_type=jnp.float32)
    return result.reshape(values.shape[:-1] + (weight.shape[1],))


def attend(queries, key_rows, value_rows, seq_first):
    full_shape = queries.shape
    split_shape = full_shape[:-1] + (HEADS, HEAD)
    query_heads = queries.reshape(split_shape)
    key_heads = key_rows.reshape(split_shape)
    value_heads = value_rows.reshape(split_shape)
    if seq_first:
        score_form = "lbhe,kbhe->bhlk"
        weigh_form = "bhlk,kbhe->lbhe"
    else:
        score_form = "blhe,bkhe->bhlk"
        weigh_form = "bhlk,bkhe->blhe"
    scores = jnp.einsum(
        score_form, query_heads, key_heads, preferred_element_type=jnp.float32
    ) * HEAD ** (-0.5)
    probs = jax.nn.softmax(scores, axis=-1).astype(jnp.bfloat16)
    mixture = jnp.einsum(weigh_form, probs, value_heads, preferred_element_type=jnp.float32)
    return mixture.astype(jnp.bfloat16).reshape(full_shape)


def transformer_layer(tokens, weights, seq_first):
    qkv_weight, out_weight, up_weight, down_weight = weights
    model_width = tokens.shape[-1]
    normed = layer_norm(tokens).astype(jnp.bfloat16)
    triple = project(normed, qkv_weight).astype(jnp.bfloat16)
    attended = attend(
        triple[..., :model_width],
        triple[..., model_width : 2 * model_width],
        triple[..., 2 * model_width :],
        seq_first,
    )
    after_attention = rounded(tokens.astype(jnp.float32) + project(attended, out_weight))
    normed_again = layer_norm(after_attention).astype(jnp.bfloat16)
    hidden = jax.nn.relu(project(normed_again, up_weight)).astype(jnp.bfloat16)
    return (after_attention.astype(jnp.float32) + project(hidden, down_weight)).astype(jnp.bfloat16)


def encode(framed, enc_weight):
    return rounded(
        jax.nn.relu(
            jnp.dot(
                framed,
                enc_weight,
                precision=lax.Precision.HIGHEST,
                preferred_element_type=jnp.float32,
            )
        )
    )


def local(
    waveform,
    enc_weight,
    intra_qkv,
    intra_out,
    intra_up,
    intra_down,
    inter_qkv,
    inter_out,
    inter_up,
    inter_down,
    mask_weight,
):
    model_width = enc_weight.shape[1]
    frames_here = waveform.shape[0] // HOP
    blocks = waveform.reshape(frames_here, HOP)
    first_block = shifted(blocks[:1], "tm", -1)
    following = jnp.concatenate([blocks[1:], first_block], axis=0)
    framed = jnp.concatenate([blocks, following], axis=1)
    encoded = encode(framed, enc_weight)
    frame_edge = shifted(encoded[:HALF], "tm", -1)
    padded = jnp.concatenate([encoded, frame_edge], axis=0)
    segment_total = frames_here // HALF
    stacked = padded.reshape(segment_total + 1, HALF, model_width)
    segmented = jnp.concatenate([stacked[:-1], stacked[1:]], axis=1)
    intra_weights = (intra_qkv, intra_out, intra_up, intra_down)
    inter_weights = (inter_qkv, inter_out, inter_up, inter_down)
    within = transformer_layer(segmented, intra_weights, False)
    within = within.reshape(segment_total, 2, HALF, model_width)
    pieces = lax.all_to_all(within, "tm", split_axis=2, concat_axis=0, tiled=True)
    row_total, item_count, spot_count, feature_count = pieces.shape
    flattened = pieces.reshape(row_total, item_count * spot_count, feature_count)
    result = transformer_layer(flattened, inter_weights, True)
    across = result.reshape(row_total, item_count, spot_count, feature_count)
    returned = lax.all_to_all(across, "tm", split_axis=0, concat_axis=2, tiled=True)
    tail_half = shifted(returned[-1:, 1], "tm", 1)
    lagged = jnp.concatenate([tail_half, returned[:-1, 1]], axis=0)
    combined = rounded(returned[:, 0].astype(jnp.float32) + lagged.astype(jnp.float32))
    combined = combined.reshape(frames_here, model_width)
    activated = combined.astype(jnp.float32)
    activated = jnp.where(activated > 0, activated, 0.25 * activated).astype(jnp.bfloat16)
    mask_values = jax.nn.relu(jnp.dot(activated, mask_weight, preferred_element_type=jnp.float32))
    mask_values = mask_values.reshape(frames_here, 2, model_width)
    separated = (mask_values * encoded.astype(jnp.float32)[:, None, :]).astype(jnp.bfloat16)
    return jnp.transpose(separated, (1, 0, 2))


LANES = 128
WITHIN_BATCH = 4
ACROSS_BATCH = 2
FINISH_ROWS = 1024
ENCODE_BLOCKS = 16
TURN_BATCH = 4
SCORE_SCALE = math.log2(math.e) * HEAD ** (-0.5)


def normalise(values):
    mean = jnp.sum(values, axis=-1, keepdims=True) * (1.0 / values.shape[-1])
    centred = values - mean
    spread = jnp.sum(centred * centred, axis=-1, keepdims=True) * (1.0 / values.shape[-1])
    return centred * lax.rsqrt(spread + 1e-05)


def round_trip(values):
    return values.astype(jnp.bfloat16).astype(jnp.float32)


def matmul(left, right):
    return jnp.dot(left, right, preferred_element_type=jnp.float32)


def put(ref, rows, value):
    for block in range(value.shape[1] // LANES):
        ref[block, rows, :] = value[:, block * LANES : (block + 1) * LANES]


def get(ref, rows):
    return jnp.concatenate([ref[block, rows, :] for block in range(ref.shape[0])], axis=1)


def attend_rows(batch):
    group = LANES // HEAD
    work = []
    for queries, keys, values in batch:
        lane_head = lax.broadcasted_iota(jnp.int32, (queries.shape[0], LANES), 1) // HEAD
        for half in range(queries.shape[1] // LANES):
            columns = slice(half * LANES, (half + 1) * LANES)
            part = queries[:, columns]
            spread = [jnp.where(lane_head == head, part, 0.0) for head in range(group)]
            spread = jnp.concatenate(spread, axis=0).astype(jnp.bfloat16)
            work.append((matmul(spread, keys[columns, :]), values[:, columns]))
    shares = []
    for scores, part in work:
        peak = jnp.max(scores, axis=-1, keepdims=True)
        weights = jnp.exp2((scores - peak) * SCORE_SCALE)
        total = jnp.sum(weights, axis=-1, keepdims=True)
        shares.append((weights.astype(jnp.bfloat16), total, part))
    mixed = [matmul(weights, part) * (1.0 / total) for weights, total, part in shares]
    results = []
    for queries, _, _ in batch:
        rows = queries.shape[0]
        lane_head = lax.broadcasted_iota(jnp.int32, (rows, LANES), 1) // HEAD
        halves = []
        for half in range(queries.shape[1] // LANES):
            block = mixed.pop(0)
            result = block[:rows]
            for head in range(1, group):
                result = jnp.where(lane_head == head, block[head * rows : (head + 1) * rows], result)
            halves.append(result)
        results.append(jnp.concatenate(halves, axis=1))
    return results


def attend_paired(batch):
    group = LANES // HEAD
    work = []
    for queries, keys, values in batch:
        lane_head = lax.broadcasted_iota(jnp.int32, queries.shape, 1) % LANES // HEAD
        spread = [jnp.where(lane_head == head, queries, 0.0) for head in range(group)]
        work.append(matmul(jnp.concatenate(spread, axis=0).astype(jnp.bfloat16), keys[...]))
    staged = []
    for scores in work:
        weights, shares = [], []
        for half in range(2):
            part = scores[:, half * LANES : (half + 1) * LANES]
            part = jnp.exp2((part - jnp.max(part, axis=-1, keepdims=True)) * SCORE_SCALE)
            weights.append(part.astype(jnp.bfloat16))
            shares.append(1.0 / jnp.sum(part, axis=-1, keepdims=True))
        staged.append((jnp.concatenate(weights, axis=1), shares))
    results = []
    for (queries, keys, values), (weights, shares) in zip(batch, staged):
        rows = queries.shape[0]
        lane_head = lax.broadcasted_iota(jnp.int32, (rows, LANES), 1) // HEAD
        mixed = matmul(weights, values[...])
        halves = []
        for half in range(2):
            block = mixed[:, half * LANES : (half + 1) * LANES] * shares[half]
            result = block[:rows]
            for head in range(1, group):
                result = jnp.where(lane_head == head, block[head * rows : (head + 1) * rows], result)
            halves.append(result)
        results.append(jnp.concatenate(halves, axis=1))
    return results


def finish_rows(tokens, attended, out_weight, up_weight, down_weight):
    after = round_trip(tokens + matmul(attended, out_weight))
    normed = normalise(after).astype(jnp.bfloat16)
    hidden = jnp.maximum(matmul(normed, up_weight), 0.0).astype(jnp.bfloat16)
    return round_trip(after + matmul(hidden, down_weight))


def core_kernel(
    place_ref,
    near_ref,
    far_ref,
    enc_ref,
    *rest,
):
    weight_sources, rest = rest[:8], rest[8:]
    act_ref, own_ref, rest = rest[0], rest[1], rest[2:]
    weight_buffers, arrivals, wave_ref, wave_arrivals, rest = rest[:8], rest[8], rest[9], rest[10], rest[11:]
    place = place_ref[0]
    chunk_rows = near_ref.shape[1]
    moves = []
    for slot in range(16):
        source = near_ref if slot < 8 else far_ref
        along = (place // 4 + slot % 4) % 4
        flipped = (place // 2 + (slot // 4) % 2) % 2
        owner = along * 4 + flipped * 2 + (place + slot // 8) % 2
        target = wave_ref.at[pl.ds(pl.multiple_of(owner * chunk_rows, chunk_rows), chunk_rows), :]
        moves.append(pltpu.make_async_copy(source.at[slot % 8], target, wave_arrivals.at[slot]))
    for move in moves:
        move.start()
    tail = wave_ref.shape[0] - 16
    wave_ref[tail:, :] = jnp.zeros((16, LANES), jnp.float32)
    copies = [
        pltpu.make_async_copy(source, buffer, arrivals.at[index])
        for index, (source, buffer) in enumerate(zip(weight_sources, weight_buffers))
    ]
    for copy in copies:
        copy.start()
    waits = [copy.wait for copy in copies] + [move.wait for move in moves]
    core_body(place, wave_ref, enc_ref, weight_buffers, waits, act_ref, own_ref, *rest)


def core_body(
    place,
    wave_ref,
    enc_ref,
    weights,
    ready_waits,
    act_ref,
    own_ref,
    band32,
    band,
    framed,
    normed,
    normed_next,
    keys,
    values,
    query_x,
    queries,
    tokens,
    attended,
    middle,
    inter_q,
    inter_k,
    inter_v,
    turned_out,
    lag,
):
    intra_qkv, intra_out, intra_up, intra_down, inter_qkv, inter_out, inter_up, inter_down = weights
    width = enc_ref.shape[1]
    rows_total = wave_ref.shape[0] - 16
    segments = rows_total // 8
    reach = HALF // 2 + HOP
    spill = LANES - reach

    band32[...] = jnp.zeros_like(band32)
    filters = enc_ref[...]
    high = round_trip(filters)
    low = round_trip(filters - high)
    for step in range(8):
        columns = slice(step * width, (step + 1) * width)
        for piece in range(2):
            sample = 8 * step + 8 * piece
            rows = slice(8 * piece, 8 * piece + 8)
            band32[sample : sample + 8, columns] = high[rows]
            band32[LANES + sample : LANES + sample + 8, columns] = high[rows]
            where = LANES + reach + sample if sample < spill else reach + sample - spill
            band32[where : where + 8, columns] = low[rows]
    for step in range(8):
        band[step] = band32[:, step * width : (step + 1) * width].astype(jnp.bfloat16)

    per_chunk = 8 * ENCODE_BLOCKS
    lane = lax.broadcasted_iota(jnp.int32, (per_chunk, LANES), 1)
    chunk_frames = ENCODE_BLOCKS * HALF
    quarter = chunk_frames // 2

    def encode_chunk(chunk, fill, drain):
        start = pl.multiple_of(chunk * per_chunk, per_chunk)
        here = wave_ref[pl.ds(start, per_chunk), :]
        after = wave_ref[pl.ds(start + 1, per_chunk), :]
        turned = jnp.where(lane < 64, pltpu.roll(here, 64, 1), pltpu.roll(after, 64, 1))
        stacked = []
        for half, samples in enumerate((here, turned)):
            coarse = round_trip(samples)
            fine = samples - coarse
            first = jnp.where(lane < reach, coarse, pltpu.roll(coarse, reach - spill, 1))
            second = jnp.where(lane < reach, fine, pltpu.roll(coarse, reach, 1))
            packed = jnp.concatenate([first, second], axis=1).astype(jnp.bfloat16)
            framed[half, pl.ds(start, per_chunk), :] = packed
            stacked.append(packed)
        rows_in = jnp.concatenate(stacked, axis=0)
        for step in range(0, 8, 2):
            if drain is not None and step % 4 == 0:
                project(chunk - 1, drain, step // 4)
            pair = [normalise(jnp.maximum(matmul(rows_in, band[step + side]), 0.0)) for side in range(2)]
            for half in range(2):
                for block in range(ENCODE_BLOCKS):
                    rows = slice(half * per_chunk + 8 * block, half * per_chunk + 8 * block + 8)
                    tile = jnp.concatenate([pair[0][rows], pair[1][rows]], axis=0).astype(jnp.bfloat16)
                    spot = block * HALF + (8 * half + step) * 8
                    fill[spot : spot + 16, :] = tile

    def project(chunk, drain, part):
        both = drain[part * quarter : (part + 1) * quarter, :]
        target = pl.ds(pl.multiple_of(chunk * chunk_frames + part * quarter, quarter), quarter)
        keys[:, target] = matmul(both, intra_qkv[:, width : 2 * width]).astype(jnp.bfloat16).T
        values[target, :] = matmul(both, intra_qkv[:, 2 * width :]).astype(jnp.bfloat16)

    for wait in ready_waits[8:]:
        wait()
    ready_waits[0]()

    def query_rows(part):
        rows = slice(part * rows_total // 2, (part + 1) * rows_total // 2)
        coded = round_trip(jnp.maximum(matmul(framed[place // 8, rows, :], band[place % 8]), 0.0))
        query_x[rows, :] = coded
        queries[rows, :] = round_trip(matmul(normalise(coded).astype(jnp.bfloat16), intra_qkv[:, :width]))

    chunks = segments // ENCODE_BLOCKS
    encode_chunk(0, normed, None)

    def encode_pair(index, carry):
        encode_chunk(2 * index + 1, normed_next, normed)
        encode_chunk(2 * index + 2, normed, normed_next)
        return carry

    lax.fori_loop(0, (chunks - 1) // 2, encode_pair, 0)
    encode_chunk(chunks - 1, normed_next, normed)
    for part in range(2):
        query_rows(part)
        project(chunks - 1, normed_next, part)
    keys[:, segments * HALF :] = jnp.zeros((width, HALF), jnp.bfloat16)
    values[segments * HALF :, :] = jnp.zeros((HALF, width), jnp.bfloat16)
    query_x[rows_total : rows_total + 8, :] = jnp.zeros((8, width), jnp.float32)
    queries[rows_total : rows_total + 8, :] = jnp.zeros((8, width), jnp.float32)
    own_rows = own_ref.shape[1]
    rows = pl.ds(pl.multiple_of(place * own_rows, own_rows), own_rows)
    for half in range(2):
        mine = framed[half, rows, :]
        for step in range(8):
            own_ref[8 * half + step] = jnp.maximum(matmul(mine, band[step]), 0.0).astype(jnp.bfloat16)

    def within_chunk(chunk, carry):
        batch, targets = [], []
        for inner in range(WITHIN_BATCH):
            segment = chunk * WITHIN_BATCH + inner
            rows = pl.ds(pl.multiple_of(segment * 8, 8), 16)
            span = pl.ds(pl.multiple_of(segment * HALF, HALF), 2 * HALF)
            target = pl.ds(pl.multiple_of(segment * 16, 16), 16)
            tokens[target, :] = query_x[rows, :]
            batch.append((queries[rows, :], keys.at[:, span], values.at[span, :]))
            targets.append(target)
        for target, result in zip(targets, attend_rows(batch)):
            attended[target, :] = result.astype(jnp.bfloat16)
        return carry

    lax.fori_loop(0, segments // WITHIN_BATCH, within_chunk, 0)

    positions = 16
    row_count = positions * segments

    for index in (1, 2, 3):
        ready_waits[index]()

    def within_finish(chunk, carry):
        rows = pl.ds(pl.multiple_of(chunk * FINISH_ROWS, FINISH_ROWS), FINISH_ROWS)
        put(middle, rows, finish_rows(tokens[rows, :], attended[rows, :], intra_out[...], intra_up[...], intra_down[...]))
        return carry

    lax.fori_loop(0, row_count // FINISH_ROWS, within_finish, 0)

    for index in (4, 5, 6, 7):
        ready_waits[index]()
    for half in range(2):
        part = slice(half * LANES, (half + 1) * LANES)
        span = slice((1 - half) * segments, (2 - half) * segments)
        inter_k[:, part, span] = jnp.zeros((positions, LANES, segments), jnp.bfloat16)
        inter_v[:, span, part] = jnp.zeros((positions, segments, LANES), jnp.bfloat16)

    def turn(chunk, carry):
        rows = pl.ds(pl.multiple_of(chunk * TURN_BATCH * segments, TURN_BATCH * segments), TURN_BATCH * segments)
        for inner in range(TURN_BATCH):
            spot = chunk * TURN_BATCH + inner
            target = pl.ds(pl.multiple_of(spot * segments, segments), segments)
            tokens[target, :] = get(middle, pl.ds(spot, segments, stride=positions))
        ready = normalise(tokens[rows, :]).astype(jnp.bfloat16)
        inter_q[rows, :] = round_trip(matmul(ready, inter_qkv[:, :width]))
        turned_keys = matmul(ready, inter_qkv[:, width : 2 * width]).astype(jnp.bfloat16).T
        new_values = matmul(ready, inter_qkv[:, 2 * width :]).astype(jnp.bfloat16)
        for inner in range(TURN_BATCH):
            spot = chunk * TURN_BATCH + inner
            source = slice(inner * segments, (inner + 1) * segments)
            for half in range(2):
                part = slice(half * LANES, (half + 1) * LANES)
                span = slice(half * segments, (half + 1) * segments)
                inter_k[spot, part, span] = turned_keys[part, source]
                inter_v[spot, span, part] = new_values[source, part]
        return carry

    lax.fori_loop(0, positions // TURN_BATCH, turn, 0)

    def across_chunk(chunk, carry):
        batch, targets = [], []
        for inner in range(ACROSS_BATCH):
            spot = chunk * ACROSS_BATCH + inner
            rows = pl.ds(pl.multiple_of(spot * segments, segments), segments)
            batch.append((inter_q[rows, :], inter_k.at[spot], inter_v.at[spot]))
            targets.append(rows)
        for target, result in zip(targets, attend_paired(batch)):
            attended[target, :] = result.astype(jnp.bfloat16)
        return carry

    lax.fori_loop(0, positions // ACROSS_BATCH, across_chunk, 0)

    def across_finish(chunk, carry):
        rows = pl.ds(pl.multiple_of(chunk * FINISH_ROWS, FINISH_ROWS), FINISH_ROWS)
        put(middle, rows, finish_rows(tokens[rows, :], attended[rows, :], inter_out[...], inter_up[...], inter_down[...]))
        return carry

    lax.fori_loop(0, row_count // FINISH_ROWS, across_finish, 0)

    lag[0:8, :] = jnp.zeros((8, width), jnp.float32)
    for spot in range(positions // 2):
        lag[8 : 8 + segments, :] = get(middle, pl.ds((spot + positions // 2) * segments, segments))
        combined = round_trip(get(middle, pl.ds(spot * segments, segments)) + lag[7 : 7 + segments, :])
        active = jnp.where(combined > 0, combined, 0.25 * combined)
        put(turned_out, pl.ds(spot, segments, stride=positions // 2), active)
    act_ref[...] = get(turned_out, slice(None)).astype(jnp.bfloat16)


def mask_kernel(act_ref, own_ref, weight_ref, out_ref, stage):
    steps, rows, _ = own_ref.shape
    for step in range(steps):
        mask = jnp.maximum(matmul(act_ref[step], weight_ref[...]), 0.0)
        put(stage, pl.ds(step, rows, stride=steps), mask * own_ref[step].astype(jnp.float32))
    out_ref[0] = get(stage, slice(None)).astype(jnp.bfloat16)


def core_call(place, near, far, enc_weight, *weights):
    width = enc_weight.shape[1]
    own_rows = near.shape[1]
    rows_total = 2 * near.shape[0] * own_rows
    segments = rows_total // 8
    row_count = 16 * segments
    vmem = pl.BlockSpec(memory_space=pltpu.VMEM)
    anywhere = pl.BlockSpec(memory_space=pl.ANY)
    return pl.pallas_call(
        core_kernel,
        out_shape=(
            jax.ShapeDtypeStruct((rows_total, width), jnp.bfloat16),
            jax.ShapeDtypeStruct((16, own_rows, width), jnp.bfloat16),
        ),
        in_specs=[pl.BlockSpec(memory_space=pltpu.SMEM)] + [anywhere] * 2 + [vmem] + [anywhere] * 8,
        out_specs=(vmem, vmem),
        scratch_shapes=[pltpu.VMEM(weight.shape, weight.dtype) for weight in weights]
        + [
            pltpu.SemaphoreType.DMA((8,)),
            pltpu.VMEM((rows_total + 16, LANES), jnp.float32),
            pltpu.SemaphoreType.DMA((16,)),
            pltpu.VMEM((2 * LANES, 8 * width), jnp.float32),
            pltpu.VMEM((8, 2 * LANES, width), jnp.bfloat16),
            pltpu.VMEM((2, rows_total, 2 * LANES), jnp.bfloat16),
            pltpu.VMEM((ENCODE_BLOCKS * HALF, width), jnp.bfloat16),
            pltpu.VMEM((ENCODE_BLOCKS * HALF, width), jnp.bfloat16),
            pltpu.VMEM((width, (segments + 1) * HALF), jnp.bfloat16),
            pltpu.VMEM(((segments + 1) * HALF, width), jnp.bfloat16),
            pltpu.VMEM((rows_total + 8, width), jnp.float32),
            pltpu.VMEM((rows_total + 8, width), jnp.float32),
            pltpu.VMEM((row_count, width), jnp.float32),
            pltpu.VMEM((row_count, width), jnp.bfloat16),
            pltpu.VMEM((width // LANES, row_count, LANES), jnp.float32),
            pltpu.VMEM((row_count, width), jnp.float32),
            pltpu.VMEM((16, width, 2 * segments), jnp.bfloat16),
            pltpu.VMEM((16, 2 * segments, width), jnp.bfloat16),
            pltpu.VMEM((width // LANES, rows_total, LANES), jnp.float32),
            pltpu.VMEM((segments + 8, width), jnp.float32),
        ],
        compiler_params=pltpu.CompilerParams(vmem_limit_bytes=60 * 1024 * 1024),
        name="core",
    )(place, near, far, enc_weight, *weights)


def gather_chunks(value, axis):
    count = lax.axis_size(axis)
    held = [value[None]]
    for ahead in range(1, 4):
        held.append(lax.ppermute(value[None], axis, [(source, (source - 4 * ahead) % count) for source in range(count)]))
    held = jnp.concatenate(held, axis=0)
    held = jnp.concatenate([held, lax.ppermute(held, axis, [(source, source ^ 2) for source in range(count)])], axis=0)
    return held, lax.ppermute(held, axis, [(source, source ^ 1) for source in range(count)])


def local_gathered(
    waveform,
    enc_weight,
    intra_qkv,
    intra_out,
    intra_up,
    intra_down,
    inter_qkv,
    inter_out,
    inter_up,
    inter_down,
    mask_weight,
):
    width = enc_weight.shape[1]
    count = lax.axis_size("tm")
    samples = waveform.reshape(-1, LANES)
    near, far = gather_chunks(samples, "tm")
    own_rows = samples.shape[0]
    place = lax.axis_index("tm").reshape(1)
    weights = (intra_qkv, intra_out, intra_up, intra_down, inter_qkv, inter_out, inter_up, inter_down)
    act, own = core_call(place, near, far, enc_weight, *weights)
    pieces = act.reshape(count, own_rows, width)
    received = lax.all_to_all(pieces, "tm", split_axis=0, concat_axis=0, tiled=True)
    whole = pl.BlockSpec(own.shape, lambda speaker: (0, 0, 0))
    return pl.pallas_call(
        mask_kernel,
        grid=(2,),
        out_shape=jax.ShapeDtypeStruct((2, 16 * own_rows, width), jnp.bfloat16),
        in_specs=[whole, whole, pl.BlockSpec((width, width), lambda speaker: (0, speaker))],
        out_specs=pl.BlockSpec((1, 16 * own_rows, width), lambda speaker: (speaker, 0, 0)),
        scratch_shapes=[pltpu.VMEM((width // LANES, 16 * own_rows, LANES), jnp.float32)],
        compiler_params=pltpu.CompilerParams(vmem_limit_bytes=32 * 1024 * 1024),
        name="mask",
    )(received, own, mask_weight)


def solution(mesh):
    body = local_gathered if mesh.shape["tm"] == 16 else local
    return jax.shard_map(
        body,
        mesh=mesh,
        in_specs=(P(("grp", "tm")), P(), P(), P(), P(), P(), P(), P(), P(), P(), P()),
        out_specs=P(None, ("grp", "tm"), None),
        check_vma=False,
    )
```
